32 devices in a mesh: groups: 2 (over y), gx: 16 (over z, x, core).
Axes of the slice: x: 2, y: 2, z: 4, core: 2. Of those that a mesh axis runs over, the one named last changes fastest.
Arguments:
- grad_out: bfloat16 [64, 4, 128, 128], P(('groups', 'gx')), parts along dimension 0, may hold values from -6 to 6
- inputs: bfloat16 [64, 4, 128, 128], P(('groups', 'gx')), parts along dimension 0, may hold values from -6 to 6
- pre_first: bfloat16 [64, 4, 128, 128], P(('groups', 'gx')), parts along dimension 0, may hold values from -6 to 6
- pre_second: bfloat16 [64, 4, 128, 128], P(('groups', 'gx')), parts along dimension 0, may hold values from -6 to 6
- filter_first: bfloat16 [3456, 128], P('gx'), may hold values from -0.109375 to 0.109375
- filter_second: bfloat16 [3456, 128], P('gx'), may hold values from -0.109375 to 0.109375
Outputs:
- grad_inputs: bfloat16 [64, 4, 128, 128], P(('groups', 'gx')), parts along dimension 0
- grad_filter_first: float32 [3456, 256], P('gx', 'groups'), parts along dimension 1
- grad_filter_second: float32 [3456, 256], P('gx', 'groups'), parts along dimension 1
The draws below stay inside these ranges and needn't reach their ends.
There are 2 independent parts, one for each index of `groups`. The reference program is written for one: setup_inputs(seed, part) draws one part's arguments, and reference() takes and returns one part's arrays. A program takes and returns all parts, laid end to end along the dimension named above; an argument that names none is the same for every part. Nothing has to cross between parts.
All inputs are finite; a program needn't handle non-finite values.
Results may differ from the reference program's by a relative error of at most 0.0058.
Values may be sent and summed in bfloat16 or wider, within the bound.
A program may use at most 64 MiB of HBM per device.

```python
import math
import jax
import jax.numpy as jnp
from jax import lax

C = 128
Y = 4
Z = 128
NX = 32


def level_of(key, dims, pieces, least, largest):
    level, own = 1.0, jax.random.fold_in(key, 6)
    for position, parts in pieces:
        heights = jnp.exp(jax.random.uniform(jax.random.fold_in(own, position), (parts,), jnp.float32, least / len(pieces), largest / len(pieces)))
        level = level * jnp.repeat(heights, dims[position] // parts).reshape([-1 if axis == position else 1 for axis in range(len(dims))])
    return level


def noise(key, dims, width, most, split=(), dtype=jnp.bfloat16):
    entries = width * jax.random.normal(key, dims, jnp.float32)
    if split:
        entries = entries * level_of(key, dims, split, -0.22, 0.18)
    return jnp.clip(entries, -most, most).astype(dtype)


def setup_inputs(seed: int = 0, part: int = 0) -> dict:
    key_of = jax.random.split(jax.random.key(seed), 7)
    part_splits = jax.random.split(jax.random.fold_in(key_of[6], part), 7)
    return {
        "grad_out": noise(part_splits[0], (NX, Y, Z, C), 1.0, 6.0, ((0, 16),)),
        "inputs": noise(part_splits[1], (NX, Y, Z, C), 1.0, 6.0, ((0, 16),)),
        "pre_first": noise(part_splits[2], (NX, Y, Z, C), 1.0, 6.0, ((0, 16),)),
        "pre_second": noise(part_splits[3], (NX, Y, Z, C), 1.0, 6.0, ((0, 16),)),
        "filter_first": noise(key_of[4], (27 * C, C), (27 * C) ** -0.5, 0.109375, ((0, 16),)),
        "filter_second": noise(key_of[5], (27 * C, C), (27 * C) ** -0.5, 0.109375, ((0, 16),)),
    }


inv_root_two = 0.7071067811865476
inv_root_twopi = 0.3989422804014327

def gelu_parts(value):
    normal_cdf = 0.5 * (1.0 + lax.erf(value * inv_root_two))
    return (value * normal_cdf, normal_cdf + value * jnp.exp(-0.5 * value * value) * inv_root_twopi)

def pad_field(field):
    return jnp.pad(field, ((1, 1), (1, 1), (1, 1), (0, 0)))

def back_data(grads, weights):
    x_cells, y_cells, z_cells, channels = grads.shape
    padded = pad_field(grads.astype(jnp.float32))
    weights = weights.astype(jnp.float32)
    running = jnp.zeros((x_cells * y_cells * z_cells, channels), jnp.float32)
    for shift_a in (-1, 0, 1):
        for shift_b in (-1, 0, 1):
            for shift_c in (-1, 0, 1):
                index = 9 * (shift_a + 1) + 3 * (shift_b + 1) + (shift_c + 1)
                tap = weights[index * channels:(index + 1) * channels]
                piece = padded[1 - shift_a:1 - shift_a + x_cells, 1 - shift_b:1 - shift_b + y_cells, 1 - shift_c:1 - shift_c + z_cells].reshape(-1, channels)
                running = running + jnp.dot(piece, tap.T, precision=lax.Precision.HIGHEST)
    return running.reshape(grads.shape)

def back_filter(saved, grads):
    x_cells, y_cells, z_cells, channels = grads.shape
    padded = pad_field(saved.astype(jnp.float32))
    flat_grads = grads.astype(jnp.float32).reshape(-1, channels)
    blocks = []
    for shift_a in (-1, 0, 1):
        for shift_b in (-1, 0, 1):
            for shift_c in (-1, 0, 1):
                piece = padded[1 + shift_a:1 + shift_a + x_cells, 1 + shift_b:1 + shift_b + y_cells, 1 + shift_c:1 + shift_c + z_cells].reshape(-1, channels)
                blocks.append(jnp.dot(piece.T, flat_grads, precision=lax.Precision.HIGHEST))
    return jnp.concatenate(blocks, axis=0)

def reference(grad_out, inputs, pre_first, pre_second, filter_first, filter_second):
    grad_scale = 1.0 / math.sqrt(NX * Y * Z)
    unused_value, slope_two = gelu_parts(pre_second.astype(jnp.float32))
    grad_two = (grad_out.astype(jnp.float32) * slope_two).astype(jnp.bfloat16)
    act_one, slope_one = gelu_parts(pre_first.astype(jnp.float32))
    act_one = act_one.astype(jnp.bfloat16)
    grad_act = back_data(grad_two, filter_second)
    filt_two = back_filter(act_one, grad_two)
    grad_one = (grad_act * slope_one).astype(jnp.bfloat16)
    grad_in = back_data(grad_one, filter_first)
    filt_one = back_filter(inputs, grad_one)
    return (grad_in.astype(jnp.bfloat16), filt_one * grad_scale, filt_two * grad_scale)
```

```python
import functools
import math

import jax
import jax.numpy as jnp
from jax import lax
from jax.experimental import pallas as pl
from jax.experimental.pallas import tpu as pltpu
from jax.sharding import PartitionSpec as P

inv_root_two = 0.7071067811865476
inv_root_twopi = 0.3989422804014327
tap_shifts = ((-1, -1), (-1, 0), (-1, 1), (0, -1), (0, 0), (0, 1), (1, -1), (1, 0), (1, 1))


def with_halo(block, sides, width):
    for axis, dim in sides:
        count = lax.axis_size(axis)
        forward = [(i, i + 1) for i in range(count - 1)]
        backward = [(target, source) for source, target in forward]
        low = lax.ppermute(
            lax.slice_in_dim(block, block.shape[dim] - width, None, axis=dim), axis, forward
        )
        high = lax.ppermute(lax.slice_in_dim(block, 0, width, axis=dim), axis, backward)
        block = jnp.concatenate([low, block, high], axis=dim)
    return block


def gelu_parts(value):
    normal_cdf = 0.5 * (1.0 + lax.erf(value * inv_root_two))
    return (value * normal_cdf, normal_cdf + value * jnp.exp(-0.5 * value * value) * inv_root_twopi)


def pad_sides(extended):
    return jnp.pad(extended, ((0, 0), (1, 1), (1, 1), (0, 0)))


def stack_taps(padded, direction, z_cells):
    return jnp.concatenate(
        [
            padded[:, :, 1 + direction * shift_z : 1 + direction * shift_z + z_cells]
            for shift_z in (-1, 0, 1)
        ],
        axis=3,
    )


def window(stacked, direction, shift_x, shift_y, x_cells, y_cells):
    start_x = 1 + direction * shift_x
    start_y = 1 + direction * shift_y
    return stacked[start_x : start_x + x_cells, start_y : start_y + y_cells]


def back_data(stacked, full_filter, shape):
    x_cells, y_cells, z_cells, channels = shape
    kernel = full_filter.reshape(3, 3, 3, channels, channels)
    running = jnp.zeros((x_cells * y_cells * z_cells, channels), jnp.float32)
    for shift_x, shift_y in tap_shifts:
        tap_matrix = jnp.transpose(kernel[shift_x + 1, shift_y + 1], (0, 2, 1)).reshape(
            3 * channels, channels
        )
        piece = window(stacked, -1, shift_x, shift_y, x_cells, y_cells).reshape(-1, 3 * channels)
        running = running + jnp.dot(piece, tap_matrix, preferred_element_type=jnp.float32)
    return running.reshape(shape)


def filter_from_inputs(stacked, grads, shape):
    x_cells, y_cells, z_cells, channels = shape
    flat_grads = grads.reshape(-1, channels)
    blocks = []
    for shift_x, shift_y in tap_shifts:
        piece = window(stacked, 1, shift_x, shift_y, x_cells, y_cells).reshape(-1, 3 * channels)
        product = lax.dot_general(
            piece, flat_grads, (((0,), (0,)), ((), ())), preferred_element_type=jnp.float32
        )
        blocks.append(product.reshape(3, channels, channels))
    return jnp.stack(blocks).reshape(27 * channels, channels)


def on_device(grad_out, inputs, pre_first, pre_second, filter_first, filter_second):
    shape = grad_out.shape
    x_cells, y_cells, z_cells, channels = shape
    full_first, full_second = (
        lax.all_gather(filter_first, "gx", axis=0, tiled=True),
        lax.all_gather(filter_second, "gx", axis=0, tiled=True),
    )
    grad_scale = 1.0 / math.sqrt(x_cells * lax.axis_size("gx") * y_cells * z_cells)
    unused_value, slope_two = gelu_parts(pre_second.astype(jnp.float32))
    grad_two = (grad_out.astype(jnp.float32) * slope_two).astype(jnp.bfloat16)
    act_one, slope_one = gelu_parts(pre_first.astype(jnp.float32))
    act_one = act_one.astype(jnp.bfloat16)
    extended_two = pad_sides(with_halo(grad_two, (("gx", 0),), 1))
    stacked_two = stack_taps(extended_two, -1, z_cells)
    grad_act = back_data(stacked_two, full_second, shape)
    extended_act = pad_sides(with_halo(act_one, (("gx", 0),), 1))
    filt_two = filter_from_inputs(stack_taps(extended_act, 1, z_cells), grad_two, shape)
    owned_two = lax.psum_scatter(filt_two * grad_scale, "gx", scatter_dimension=0, tiled=True)
    grad_one = (grad_act * slope_one).astype(jnp.bfloat16)
    extended_one = pad_sides(with_halo(grad_one, (("gx", 0),), 1))
    stacked_one = stack_taps(extended_one, -1, z_cells)
    grad_in = back_data(stacked_one, full_first, shape).astype(jnp.bfloat16)
    extended_in = pad_sides(with_halo(inputs, (("gx", 0),), 1))
    filt_one = filter_from_inputs(stack_taps(extended_in, 1, z_cells), grad_one, shape)
    owned_one = lax.psum_scatter(filt_one * grad_scale, "gx", scatter_dimension=0, tiled=True)
    return (grad_in, owned_one, owned_two)


MESH = pl.DeviceIdType.MESH
sub = 8


def shift_z(block, shift):
    if shift == 0:
        return block
    cells = block.shape[0]
    row = lax.broadcasted_iota(jnp.int32, block.shape, 0)
    edge = 0 if shift > 0 else cells - 1
    return jnp.where(row == edge, 0.0, pltpu.roll(block, shift % cells, 0))


def kernel(
    n, go, xin, p1, p2, f1, f2, gin, own1, own2,
    fbuf, wbuf, gext, abuf, ahalo, sat, gcat, slope, part, s1, r1, s2, r2, s3, r3,
    halo_s, halo_r, agz_s, agz_r, agx_s, agx_r, agc_s, agc_r,
    rs1_s, rs1_r, rs2_s, rs2_r, rs3_s, rs3_r,
):
    xs, ys, zs, ch = go.shape
    units = f1.shape[0]
    hi = n // 4
    group, me = lax.axis_index("groups"), lax.axis_index("gx")
    core = me % 2
    mid = (me // 2) % 2
    top = me // 4
    partner = me + 1 - 2 * core
    across = me + 2 - 4 * mid

    def owner(t, m, c):
        return (t * 2 + m) * 2 + c

    def chunk(t, m, c):
        return pl.ds(owner(t, m, c) * units, units)

    def ahead(d):
        return lax.rem(top + d, hi)

    def behind(d):
        return lax.rem(top + hi - d, hi)

    sent = []

    def push(src, dst, send, recv, target):
        copy = pltpu.make_async_remote_copy(
            src_ref=src, dst_ref=dst, send_sem=send, recv_sem=recv,
            device_id=(group, target), device_id_type=MESH,
        )
        copy.start()
        sent.append(copy)

    def arrive(dst, send, recv):
        pltpu.make_async_remote_copy(
            src_ref=dst, dst_ref=dst, send_sem=send, recv_sem=recv,
            device_id=(group, partner), device_id_type=MESH,
        ).wait_recv()

    barrier = pltpu.get_barrier_semaphore()
    peers = [partner, across, lax.rem(me + 1, n), lax.rem(me + n - 1, n)]
    peers += [owner(ahead(d), mid, core) for d in range(1, hi)]
    for peer in peers:
        pl.semaphore_signal(barrier, inc=1, device_id=(group, peer), device_id_type=MESH)
    pl.semaphore_wait(barrier, len(peers))

    filters = (f2, f1)

    def gather_own(f):
        mine = fbuf.at[f, chunk(top, mid, core)]
        for d in range(1, hi):
            push(filters[f], mine, agz_s.at[f, d], agz_r.at[f, d], owner(ahead(d), mid, core))
        push(filters[f], mine, agx_s.at[f, 0], agx_r.at[f, 0], across)
        push(filters[f], mine, agc_s.at[f, 0], agc_r.at[f, 0], partner)
        fbuf[f, chunk(top, mid, core)] = filters[f][...]

    def gather_top(f):
        for d in range(1, hi):
            got = fbuf.at[f, chunk(behind(d), mid, core)]
            arrive(got, agz_s.at[f, d], agz_r.at[f, d])
            push(got, got, agx_s.at[f, d], agx_r.at[f, d], across)
            push(got, got, agc_s.at[f, d], agc_r.at[f, d], partner)

    def gather_mid(f):
        for d in range(hi):
            got = fbuf.at[f, chunk(behind(d), 1 - mid, core)]
            arrive(got, agx_s.at[f, d], agx_r.at[f, d])
            push(got, got, agc_s.at[f, hi + d], agc_r.at[f, hi + d], partner)

    def gather_core(f):
        for m in range(2):
            for d in range(hi):
                which = mid if m == 0 else 1 - mid
                got = fbuf.at[f, chunk(behind(d), which, 1 - core)]
                arrive(got, agc_s.at[f, m * hi + d], agc_r.at[f, m * hi + d])
        taps = 3 * ch // sub
        for ab in range(9):
            rows = fbuf[f, ab * taps : (ab + 1) * taps].astype(jnp.float32)
            wbuf[f, :, ab * ch : (ab + 1) * ch] = rows.reshape(3 * ch, ch).astype(jnp.bfloat16)

    def halo_copy(h, first, last, low, high):
        to_left = pltpu.make_async_remote_copy(
            src_ref=first, dst_ref=high, send_sem=halo_s.at[h, 0], recv_sem=halo_r.at[h, 1],
            device_id=(group, lax.rem(me + n - 1, n)), device_id_type=MESH,
        )
        to_right = pltpu.make_async_remote_copy(
            src_ref=last, dst_ref=low, send_sem=halo_s.at[h, 1], recv_sem=halo_r.at[h, 0],
            device_id=(group, lax.rem(me + 1, n)), device_id_type=MESH,
        )

        @pl.when(me > 0)
        def _():
            to_left.start()

        @pl.when(me < n - 1)
        def _():
            to_right.start()

        return to_left, to_right, low, high, h

    def halo_wait(halo):
        _, _, low, high, h = halo

        @pl.when(me > 0)
        def _():
            arrive(low, halo_s.at[h, 0], halo_r.at[h, 0])

        @pl.when(me == 0)
        def _():
            low[...] = jnp.zeros(low.shape, low.dtype)

        @pl.when(me < n - 1)
        def _():
            arrive(high, halo_s.at[h, 1], halo_r.at[h, 1])

        @pl.when(me == n - 1)
        def _():
            high[...] = jnp.zeros(high.shape, high.dtype)

    def grad_halo(h, f):
        inner = pl.ds(1, ys)
        return halo_copy(
            h, gext.at[f, 1, inner], gext.at[f, xs, inner],
            gext.at[f, 0, inner], gext.at[f, xs + 1, inner],
        )

    def saved_halo(h, s, block):
        return halo_copy(h, block.at[0], block.at[xs - 1], ahalo.at[s, 0], ahalo.at[s, 1])

    def keep_grad(f, x, y, value):
        gext[f, x + 1, y + 1] = value.astype(jnp.bfloat16)
        start = pl.multiple_of((x * ys + y) * zs, zs)
        for c in (-1, 0, 1):
            gcat[f, pl.ds(start, zs), (c + 1) * ch : (c + 2) * ch] = shift_z(value, c).astype(
                jnp.bfloat16
            )

    def turn(s, layer, block):
        for y in range(ys):
            sat[s, layer, :, (y + 1) * zs : (y + 2) * zs] = block[y].T

    def filter_terms(s):
        for a in range(3):
            lhs = jnp.concatenate(
                [
                    jnp.concatenate(
                        [sat[s, x + a, :, b * zs : (b + ys) * zs] for x in range(xs)], axis=1
                    )
                    for b in range(3)
                ],
                axis=0,
            )
            out = jnp.dot(lhs, gcat[s], preferred_element_type=jnp.float32)
            per = ch // sub
            for b in range(3):
                for c in range(3):
                    at = (9 * a + 3 * b + c) * per
                    part[s, at : at + per] = out[
                        b * ch : (b + 1) * ch, c * ch : (c + 1) * ch
                    ].reshape(per, sub, ch)

    def scatter_core(s):
        for m in range(2):
            which = 1 - mid if m == 0 else mid
            for t in range(hi):
                s1[s, m, t] = part[s, chunk(t, which, 1 - core)].astype(jnp.bfloat16)
            push(s1.at[s, m], r1.at[s, m], rs1_s.at[s, m], rs1_r.at[s, m], partner)

    def scatter_mid(s):
        arrive(r1.at[s, 0], rs1_s.at[s, 0], rs1_r.at[s, 0])
        for t in range(hi):
            s2[s, t] = (
                part[s, chunk(t, 1 - mid, core)] + r1[s, 0, t].astype(jnp.float32)
            ).astype(jnp.bfloat16)
        push(s2.at[s], r2.at[s], rs2_s.at[s], rs2_r.at[s], across)

    def total(s, t):
        return (
            part[s, chunk(t, mid, core)]
            + r1[s, 1, t].astype(jnp.float32)
            + r2[s, t].astype(jnp.float32)
        )

    def scatter_top(s):
        arrive(r1.at[s, 1], rs1_s.at[s, 1], rs1_r.at[s, 1])
        arrive(r2.at[s], rs2_s.at[s], rs2_r.at[s])
        for d in range(1, hi):
            s3[s, d] = total(s, ahead(d)).astype(jnp.bfloat16)
            push(
                s3.at[s, d], r3.at[s, d], rs3_s.at[s, d], rs3_r.at[s, d],
                owner(ahead(d), mid, core),
            )

    def scatter_end(s, out):
        value = total(s, top)
        for d in range(1, hi):
            arrive(r3.at[s, d], rs3_s.at[s, d], rs3_r.at[s, d])
            value = value + r3[s, d].astype(jnp.float32)
        out[...] = value * (1.0 / math.sqrt(xs * n * ys * zs))

    def layer_back(f, x):
        lhs = jnp.concatenate(
            [
                gext[f, x + 1 - a, 1 - b : 1 - b + ys].reshape(ys * zs, ch)
                for a in (-1, 0, 1)
                for b in (-1, 0, 1)
            ],
            axis=1,
        )
        wide = lax.dot_general(
            lhs, wbuf[f], (((1,), (1,)), ((), ())), preferred_element_type=jnp.float32
        )
        rows = []
        for y in range(ys):
            block = wide[y * zs : (y + 1) * zs]
            rows.append(
                shift_z(block[:, :ch], -1) + block[:, ch : 2 * ch] + shift_z(block[:, 2 * ch :], 1)
            )
        return rows

    gather_own(0)

    for f in range(2):
        for x in range(xs + 2):
            for y in (0, ys + 1):
                gext[f, x, y] = jnp.zeros((zs, ch), jnp.bfloat16)
                sat[f, x, :, y * zs : (y + 1) * zs] = jnp.zeros((ch, zs), jnp.bfloat16)

    @pl.loop(0, xs * ys)
    def _(i):
        x, y = i // ys, i % ys
        _, slope_two = gelu_parts(p2[x, y].astype(jnp.float32))
        keep_grad(0, x, y, go[x, y].astype(jnp.float32) * slope_two)
        act, slope_one = gelu_parts(p1[x, y].astype(jnp.float32))
        abuf[x, y] = act.astype(jnp.bfloat16)
        slope[x, y] = slope_one

    halo_act = saved_halo(0, 0, abuf)
    halo_two = grad_halo(1, 0)
    gather_top(0)
    halo_in = saved_halo(2, 1, xin)
    gather_own(1)
    for x in range(xs):
        turn(0, x + 1, abuf[x])
        turn(1, x + 1, xin[x])
    gather_mid(0)
    halo_wait(halo_act)
    turn(0, 0, ahalo[0, 0])
    turn(0, xs + 1, ahalo[0, 1])
    filter_terms(0)
    scatter_core(0)
    gather_top(1)
    gather_core(0)
    halo_wait(halo_two)
    scatter_mid(0)
    for x in range(xs):
        for y, value in enumerate(layer_back(0, x)):
            keep_grad(1, x, y, value * slope[x, y])
    halo_one = grad_halo(3, 1)
    gather_mid(1)
    halo_wait(halo_in)
    turn(1, 0, ahalo[1, 0])
    turn(1, xs + 1, ahalo[1, 1])
    filter_terms(1)
    scatter_core(1)
    scatter_top(0)
    gather_core(1)
    scatter_mid(1)
    halo_wait(halo_one)
    for x in range(xs):
        for y, value in enumerate(layer_back(1, x)):
            gin[x, y] = value.astype(jnp.bfloat16)
        if x == 0:
            scatter_top(1)
    scatter_end(0, own2)
    scatter_end(1, own1)
    for copy in sent:
        copy.wait_send()
    for halo in (halo_act, halo_two, halo_in, halo_one):

        @pl.when(me > 0)
        def _():
            halo[0].wait_send()

        @pl.when(me < n - 1)
        def _():
            halo[1].wait_send()


def fused(grad_out, inputs, pre_first, pre_second, filter_first, filter_second):
    n = lax.axis_size("gx")
    xs, ys, zs, ch = grad_out.shape
    rows = filter_first.shape[0]
    if rows % sub or n % 4 or n < 8:
        return on_device(grad_out, inputs, pre_first, pre_second, filter_first, filter_second)
    units, hi, bf = rows // sub, n // 4, jnp.bfloat16
    dma = pltpu.SemaphoreType.DMA
    piece = (units, sub, ch)
    gin, own1, own2 = pl.pallas_call(
        functools.partial(kernel, n),
        out_shape=(
            jax.ShapeDtypeStruct(grad_out.shape, bf),
            jax.ShapeDtypeStruct(piece, jnp.float32),
            jax.ShapeDtypeStruct(piece, jnp.float32),
        ),
        in_specs=[pl.BlockSpec(memory_space=pltpu.VMEM)] * 6,
        out_specs=[pl.BlockSpec(memory_space=pltpu.VMEM)] * 3,
        scratch_shapes=[
            pltpu.VMEM((2, n * units, sub, ch), bf),
            pltpu.VMEM((2, 3 * ch, 9 * ch), bf),
            pltpu.VMEM((2, xs + 2, ys + 2, zs, ch), bf),
            pltpu.VMEM((xs, ys, zs, ch), bf),
            pltpu.VMEM((2, 2, ys, zs, ch), bf),
            pltpu.VMEM((2, xs + 2, ch, (ys + 2) * zs), bf),
            pltpu.VMEM((2, xs * ys * zs, 3 * ch), bf),
            pltpu.VMEM((xs, ys, zs, ch), jnp.float32),
            pltpu.VMEM((2, n * units, sub, ch), jnp.float32),
            pltpu.VMEM((2, 2, hi) + piece, bf),
            pltpu.VMEM((2, 2, hi) + piece, bf),
            pltpu.VMEM((2, hi) + piece, bf),
            pltpu.VMEM((2, hi) + piece, bf),
            pltpu.VMEM((2, hi) + piece, bf),
            pltpu.VMEM((2, hi) + piece, bf),
            dma((4, 2)), dma((4, 2)),
            dma((2, hi)), dma((2, hi)),
            dma((2, hi)), dma((2, hi)),
            dma((2, 2 * hi)), dma((2, 2 * hi)),
            dma((2, 2)), dma((2, 2)),
            dma((2,)), dma((2,)),
            dma((2, hi)), dma((2, hi)),
        ],
        compiler_params=pltpu.CompilerParams(collective_id=0, has_side_effects=True),
    )(
        grad_out, inputs, pre_first, pre_second,
        filter_first.reshape(piece), filter_second.reshape(piece),
    )
    return gin, own1.reshape(rows, ch), own2.reshape(rows, ch)


def solution(mesh):
    return jax.shard_map(
        fused,
        mesh=mesh,
        in_specs=(
            P(("groups", "gx"), None, None, None),
            P(("groups", "gx"), None, None, None),
            P(("groups", "gx"), None, None, None),
            P(("groups", "gx"), None, None, None),
            P("gx", None),
            P("gx", None),
        ),
        out_specs=(P(("groups", "gx"), None, None, None), P("gx", "groups"), P("gx", "groups")),
        check_vma=False,
    )
```

```python
import functools
import math

import jax
import jax.numpy as jnp
from jax import lax
from jax.experimental import pallas as pl
from jax.experimental.pallas import tpu as pltpu
from jax.sharding import PartitionSpec as P

inv_root_two = 0.7071067811865476
inv_root_twopi = 0.3989422804014327
tap_shifts = ((-1, -1), (-1, 0), (-1, 1), (0, -1), (0, 0), (0, 1), (1, -1), (1, 0), (1, 1))


def with_halo(block, sides, width):
    for axis, dim in sides:
        count = lax.axis_size(axis)
        forward = [(i, i + 1) for i in range(count - 1)]
        backward = [(target, source) for source, target in forward]
        low = lax.ppermute(
            lax.slice_in_dim(block, block.shape[dim] - width, None, axis=dim), axis, forward
        )
        high = lax.ppermute(lax.slice_in_dim(block, 0, width, axis=dim), axis, backward)
        block = jnp.concatenate([low, block, high], axis=dim)
    return block


def gelu_parts(value):
    normal_cdf = 0.5 * (1.0 + lax.erf(value * inv_root_two))
    return (value * normal_cdf, normal_cdf + value * jnp.exp(-0.5 * value * value) * inv_root_twopi)


def pad_sides(extended):
    return jnp.pad(extended, ((0, 0), (1, 1), (1, 1), (0, 0)))


def stack_taps(padded, direction, z_cells):
    return jnp.concatenate(
        [
            padded[:, :, 1 + direction * shift_z : 1 + direction * shift_z + z_cells]
            for shift_z in (-1, 0, 1)
        ],
        axis=3,
    )


def window(stacked, direction, shift_x, shift_y, x_cells, y_cells):
    start_x = 1 + direction * shift_x
    start_y = 1 + direction * shift_y
    return stacked[start_x : start_x + x_cells, start_y : start_y + y_cells]


def back_data(stacked, full_filter, shape):
    x_cells, y_cells, z_cells, channels = shape
    kernel = full_filter.reshape(3, 3, 3, channels, channels)
    running = jnp.zeros((x_cells * y_cells * z_cells, channels), jnp.float32)
    for shift_x, shift_y in tap_shifts:
        tap_matrix = jnp.transpose(kernel[shift_x + 1, shift_y + 1], (0, 2, 1)).reshape(
            3 * channels, channels
        )
        piece = window(stacked, -1, shift_x, shift_y, x_cells, y_cells).reshape(-1, 3 * channels)
        running = running + jnp.dot(piece, tap_matrix, preferred_element_type=jnp.float32)
    return running.reshape(shape)


def filter_from_inputs(stacked, grads, shape):
    x_cells, y_cells, z_cells, channels = shape
    flat_grads = grads.reshape(-1, channels)
    blocks = []
    for shift_x, shift_y in tap_shifts:
        piece = window(stacked, 1, shift_x, shift_y, x_cells, y_cells).reshape(-1, 3 * channels)
        product = lax.dot_general(
            piece, flat_grads, (((0,), (0,)), ((), ())), preferred_element_type=jnp.float32
        )
        blocks.append(product.reshape(3, channels, channels))
    return jnp.stack(blocks).reshape(27 * channels, channels)


def on_device(grad_out, inputs, pre_first, pre_second, filter_first, filter_second):
    shape = grad_out.shape
    x_cells, y_cells, z_cells, channels = shape
    full_first, full_second = (
        lax.all_gather(filter_first, "gx", axis=0, tiled=True),
        lax.all_gather(filter_second, "gx", axis=0, tiled=True),
    )
    grad_scale = 1.0 / math.sqrt(x_cells * lax.axis_size("gx") * y_cells * z_cells)
    unused_value, slope_two = gelu_parts(pre_second.astype(jnp.float32))
    grad_two = (grad_out.astype(jnp.float32) * slope_two).astype(jnp.bfloat16)
    act_one, slope_one = gelu_parts(pre_first.astype(jnp.float32))
    act_one = act_one.astype(jnp.bfloat16)
    extended_two = pad_sides(with_halo(grad_two, (("gx", 0),), 1))
    stacked_two = stack_taps(extended_two, -1, z_cells)
    grad_act = back_data(stacked_two, full_second, shape)
    extended_act = pad_sides(with_halo(act_one, (("gx", 0),), 1))
    filt_two = filter_from_inputs(stack_taps(extended_act, 1, z_cells), grad_two, shape)
    owned_two = lax.psum_scatter(filt_two * grad_scale, "gx", scatter_dimension=0, tiled=True)
    grad_one = (grad_act * slope_one).astype(jnp.bfloat16)
    extended_one = pad_sides(with_halo(grad_one, (("gx", 0),), 1))
    stacked_one = stack_taps(extended_one, -1, z_cells)
    grad_in = back_data(stacked_one, full_first, shape).astype(jnp.bfloat16)
    extended_in = pad_sides(with_halo(inputs, (("gx", 0),), 1))
    filt_one = filter_from_inputs(stack_taps(extended_in, 1, z_cells), grad_one, shape)
    owned_one = lax.psum_scatter(filt_one * grad_scale, "gx", scatter_dimension=0, tiled=True)
    return (grad_in, owned_one, owned_two)


MESH = pl.DeviceIdType.MESH
sub = 8


def shift_z(block, shift):
    if shift == 0:
        return block
    cells = block.shape[0]
    row = lax.broadcasted_iota(jnp.int32, block.shape, 0)
    edge = 0 if shift > 0 else cells - 1
    return jnp.where(row == edge, 0.0, pltpu.roll(block, shift % cells, 0))


def kernel(
    n, go, xin, p1, p2, f1, f2, gin, own1, own2,
    fbuf, wbuf, gext, abuf, ahalo, sat, gcat, slope, part, s1, r1, s2, r2, s3, r3,
    halo_s, halo_r, agz_s, agz_r, agx_s, agx_r, agy_s, agy_r, agc_s, agc_r,
    rs1_s, rs1_r, rs2_s, rs2_r, rs3_s, rs3_r,
):
    xs, ys, zs, ch = go.shape
    units = f1.shape[0]
    hi = n // 4
    group, me = lax.axis_index("groups"), lax.axis_index("gx")
    core = me % 2
    mid = (me // 2) % 2
    top = me // 4
    partner = me + 1 - 2 * core
    across = me + 2 - 4 * mid

    def owner(t, m, c):
        return (t * 2 + m) * 2 + c

    def chunk(t, m, c):
        return pl.ds(owner(t, m, c) * units, units)

    def ahead(d):
        return lax.rem(top + d, hi)

    def behind(d):
        return lax.rem(top + hi - d, hi)

    lead = core == group
    sent = []

    def push(src, dst, send, recv, target, plane=group, keep=True):
        copy = pltpu.make_async_remote_copy(
            src_ref=src, dst_ref=dst, send_sem=send, recv_sem=recv,
            device_id=(plane, target), device_id_type=MESH,
        )
        copy.start()
        if keep:
            sent.append(copy)

    def arrive(dst, send, recv):
        pltpu.make_async_remote_copy(
            src_ref=dst, dst_ref=dst, send_sem=send, recv_sem=recv,
            device_id=(group, partner), device_id_type=MESH,
        ).wait_recv()

    barrier = pltpu.get_barrier_semaphore()
    peers = [partner, across, lax.rem(me + 1, n), lax.rem(me + n - 1, n)]
    peers += [owner(ahead(d), mid, core) for d in range(1, hi)]
    for peer in peers:
        pl.semaphore_signal(barrier, inc=1, device_id=(group, peer), device_id_type=MESH)
    pl.semaphore_signal(barrier, inc=1, device_id=(1 - group, me), device_id_type=MESH)
    pl.semaphore_wait(barrier, len(peers) + 1)

    filters = (f2, f1)

    def gather_own(f):
        mine = fbuf.at[f, chunk(top, mid, core)]
        src = filters[f]
        push(src, mine, agc_s.at[f, 0], agc_r.at[f, 0], partner)

        @pl.when(lead)
        def _():
            for d in range(1, hi):
                push(
                    src, mine, agz_s.at[f, d], agz_r.at[f, d],
                    owner(ahead(d), mid, core), keep=False,
                )
            push(src, mine, agx_s.at[f, 0], agx_r.at[f, 0], across, keep=False)

        fbuf[f, chunk(top, mid, core)] = src[...]

    def hand_on(f, got, k):
        push(got, got, agy_s.at[f, k], agy_r.at[f, k], me, 1 - group, False)
        push(got, got, agc_s.at[f, k], agc_r.at[f, k], partner, keep=False)

    def gather_top(f):
        @pl.when(lead)
        def _():
            for d in range(1, hi):
                got = fbuf.at[f, chunk(behind(d), mid, core)]
                arrive(got, agz_s.at[f, d], agz_r.at[f, d])
                push(got, got, agx_s.at[f, d], agx_r.at[f, d], across, keep=False)
                hand_on(f, got, d)

    def gather_mid(f):
        @pl.when(lead)
        def _():
            for d in range(hi):
                got = fbuf.at[f, chunk(behind(d), 1 - mid, core)]
                arrive(got, agx_s.at[f, d], agx_r.at[f, d])
                hand_on(f, got, hi + d)

    def gather_follow(f):
        @pl.when(jnp.logical_not(lead))
        def _():
            for k in range(1, 2 * hi):
                which = mid if k < hi else 1 - mid
                got = fbuf.at[f, chunk(behind(k % hi), which, core)]
                arrive(got, agy_s.at[f, k], agy_r.at[f, k])
                push(got, got, agc_s.at[f, k], agc_r.at[f, k], partner, keep=False)

    def gather_core(f):
        for m in range(2):
            for d in range(hi):
                which = mid if m == 0 else 1 - mid
                got = fbuf.at[f, chunk(behind(d), which, 1 - core)]
                arrive(got, agc_s.at[f, m * hi + d], agc_r.at[f, m * hi + d])
        taps = 3 * ch // sub
        for ab in range(9):
            rows = fbuf[f, ab * taps : (ab + 1) * taps].astype(jnp.float32)
            wbuf[f, :, ab * ch : (ab + 1) * ch] = rows.reshape(3 * ch, ch).astype(jnp.bfloat16)

    def halo_copy(h, first, last, low, high):
        to_left = pltpu.make_async_remote_copy(
            src_ref=first, dst_ref=high, send_sem=halo_s.at[h, 0], recv_sem=halo_r.at[h, 1],
            device_id=(group, lax.rem(me + n - 1, n)), device_id_type=MESH,
        )
        to_right = pltpu.make_async_remote_copy(
            src_ref=last, dst_ref=low, send_sem=halo_s.at[h, 1], recv_sem=halo_r.at[h, 0],
            device_id=(group, lax.rem(me + 1, n)), device_id_type=MESH,
        )

        @pl.when(me > 0)
        def _():
            to_left.start()

        @pl.when(me < n - 1)
        def _():
            to_right.start()

        return to_left, to_right, low, high, h

    def halo_wait(halo):
        _, _, low, high, h = halo

        @pl.when(me > 0)
        def _():
            arrive(low, halo_s.at[h, 0], halo_r.at[h, 0])

        @pl.when(me == 0)
        def _():
            low[...] = jnp.zeros(low.shape, low.dtype)

        @pl.when(me < n - 1)
        def _():
            arrive(high, halo_s.at[h, 1], halo_r.at[h, 1])

        @pl.when(me == n - 1)
        def _():
            high[...] = jnp.zeros(high.shape, high.dtype)

    def grad_halo(h, f):
        inner = pl.ds(1, ys)
        return halo_copy(
            h, gext.at[f, 1, inner], gext.at[f, xs, inner],
            gext.at[f, 0, inner], gext.at[f, xs + 1, inner],
        )

    def saved_halo(h, s, block):
        return halo_copy(h, block.at[0], block.at[xs - 1], ahalo.at[s, 0], ahalo.at[s, 1])

    def keep_shifts(f, x, y, value):
        for c in (-1, 0, 1):
            gcat[f, x + 1, y + 1, :, (c + 1) * ch : (c + 2) * ch] = shift_z(value, c).astype(
                jnp.bfloat16
            )

    def keep_grad(f, x, y, value):
        gext[f, x + 1, y + 1] = value.astype(jnp.bfloat16)
        keep_shifts(f, x, y, value)

    def halo_shifts(f):
        for x in (-1, xs):
            for y in range(ys):
                keep_shifts(f, x, y, gext[f, x + 1, y + 1].astype(jnp.float32))

    def turn(s, layer, block):
        for y in range(ys):
            sat[s, layer, :, (y + 1) * zs : (y + 2) * zs] = block[y].T

    def filter_terms(s):
        for a in range(3):
            lhs = jnp.concatenate(
                [
                    jnp.concatenate(
                        [sat[s, x + a, :, b * zs : (b + ys) * zs] for x in range(xs)], axis=1
                    )
                    for b in range(3)
                ],
                axis=0,
            )
            rhs = gcat[s, 1 : xs + 1, 1 : ys + 1].reshape(xs * ys * zs, 3 * ch)
            out = jnp.dot(lhs, rhs, preferred_element_type=jnp.float32)
            per = ch // sub
            for b in range(3):
                for c in range(3):
                    at = (9 * a + 3 * b + c) * per
                    part[s, at : at + per] = out[
                        b * ch : (b + 1) * ch, c * ch : (c + 1) * ch
                    ].reshape(per, sub, ch)

    def filter_terms_halo(s):
        lhs = jnp.concatenate([sat[s, x + 1, :, zs : (ys + 1) * zs] for x in range(xs)], axis=1)
        per = ch // sub
        for a in (0, -1, 1):
            for b in (-1, 0, 1):
                rhs = gcat[s, 1 - a : 1 - a + xs, 1 - b : 1 - b + ys].reshape(
                    xs * ys * zs, 3 * ch
                )
                out = jnp.dot(lhs, rhs, preferred_element_type=jnp.float32)
                for c in range(3):
                    at = (9 * (a + 1) + 3 * (b + 1) + c) * per
                    part[s, at : at + per] = out[:, c * ch : (c + 1) * ch].reshape(per, sub, ch)

    def scatter_core(s):
        for m in range(2):
            which = 1 - mid if m == 0 else mid
            for t in range(hi):
                s1[s, m, t] = part[s, chunk(t, which, 1 - core)].astype(jnp.bfloat16)
            push(s1.at[s, m], r1.at[s, m], rs1_s.at[s, m], rs1_r.at[s, m], partner)

    def scatter_mid(s):
        arrive(r1.at[s, 0], rs1_s.at[s, 0], rs1_r.at[s, 0])
        for d in [*range(1, hi), 0]:
            t = ahead(d)
            s2[s, t] = (
                part[s, chunk(t, 1 - mid, core)] + r1[s, 0, t].astype(jnp.float32)
            ).astype(jnp.bfloat16)
            push(s2.at[s, t], r2.at[s, t], rs2_s.at[s, d], rs2_r.at[s, d], across)

    def total(s, t):
        return (
            part[s, chunk(t, mid, core)]
            + r1[s, 1, t].astype(jnp.float32)
            + r2[s, t].astype(jnp.float32)
        )

    def scatter_top(s):
        arrive(r1.at[s, 1], rs1_s.at[s, 1], rs1_r.at[s, 1])
        for d in range(1, hi):
            arrive(r2.at[s, ahead(d)], rs2_s.at[s, d], rs2_r.at[s, d])
            s3[s, d] = total(s, ahead(d)).astype(jnp.bfloat16)
            push(
                s3.at[s, d], r3.at[s, d], rs3_s.at[s, d], rs3_r.at[s, d],
                owner(ahead(d), mid, core),
            )

    def scatter_end(s, out):
        arrive(r2.at[s, top], rs2_s.at[s, 0], rs2_r.at[s, 0])
        value = total(s, top)
        for d in range(1, hi):
            arrive(r3.at[s, d], rs3_s.at[s, d], rs3_r.at[s, d])
            value = value + r3[s, d].astype(jnp.float32)
        out[...] = value * (1.0 / math.sqrt(xs * n * ys * zs))

    def layer_back(f, x):
        lhs = jnp.concatenate(
            [
                gext[f, x + 1 - a, 1 - b : 1 - b + ys].reshape(ys * zs, ch)
                for a in (-1, 0, 1)
                for b in (-1, 0, 1)
            ],
            axis=1,
        )
        wide = lax.dot_general(
            lhs, wbuf[f], (((1,), (1,)), ((), ())), preferred_element_type=jnp.float32
        )
        rows = []
        for y in range(ys):
            block = wide[y * zs : (y + 1) * zs]
            rows.append(
                shift_z(block[:, :ch], -1) + block[:, ch : 2 * ch] + shift_z(block[:, 2 * ch :], 1)
            )
        return rows

    gather_own(0)

    for f in range(2):
        for x in range(xs + 2):
            for y in (0, ys + 1):
                gext[f, x, y] = jnp.zeros((zs, ch), jnp.bfloat16)
                gcat[f, x, y] = jnp.zeros((zs, 3 * ch), jnp.bfloat16)
                sat[f, x, :, y * zs : (y + 1) * zs] = jnp.zeros((ch, zs), jnp.bfloat16)

    @pl.loop(0, xs * ys)
    def _(i):
        x, y = i // ys, i % ys
        _, slope_two = gelu_parts(p2[x, y].astype(jnp.float32))
        keep_grad(0, x, y, go[x, y].astype(jnp.float32) * slope_two)
        act, slope_one = gelu_parts(p1[x, y].astype(jnp.float32))
        abuf[x, y] = act.astype(jnp.bfloat16)
        slope[x, y] = slope_one

    halo_two = grad_halo(1, 0)
    gather_top(0)
    halo_in = saved_halo(0, 0, xin)
    for x in range(xs):
        turn(0, x + 1, abuf[x])
        turn(1, x + 1, xin[x])
    gather_mid(0)
    gather_own(1)
    gather_follow(0)
    halo_wait(halo_two)
    halo_shifts(0)
    filter_terms_halo(0)
    scatter_core(0)
    gather_core(0)
    gather_top(1)
    scatter_mid(0)
    for x in range(xs):
        for y, value in enumerate(layer_back(0, x)):
            keep_grad(1, x, y, value * slope[x, y])
    halo_one = grad_halo(2, 1)
    halo_wait(halo_in)
    turn(1, 0, ahalo[0, 0])
    turn(1, xs + 1, ahalo[0, 1])
    filter_terms(1)
    scatter_core(1)
    gather_mid(1)
    scatter_top(0)
    scatter_mid(1)
    gather_follow(1)
    scatter_top(1)
    gather_core(1)
    halo_wait(halo_one)
    for x in range(xs):
        for y, value in enumerate(layer_back(1, x)):
            gin[x, y] = value.astype(jnp.bfloat16)
    scatter_end(0, own2)
    scatter_end(1, own1)
    for copy in sent:
        copy.wait_send()

    def left(f, send):
        pltpu.make_async_remote_copy(
            src_ref=filters[f], dst_ref=filters[f], send_sem=send, recv_sem=agc_r.at[f, 0],
            device_id=(group, partner), device_id_type=MESH,
        ).wait_send()

    for f in range(2):
        for k in range(1, 2 * hi):
            left(f, agc_s.at[f, k])

    @pl.when(lead)
    def _():
        for f in range(2):
            for d in range(1, hi):
                left(f, agz_s.at[f, d])
            for d in range(hi):
                left(f, agx_s.at[f, d])
            for k in range(1, 2 * hi):
                left(f, agy_s.at[f, k])

    for halo in (halo_two, halo_in, halo_one):

        @pl.when(me > 0)
        def _():
            halo[0].wait_send()

        @pl.when(me < n - 1)
        def _():
            halo[1].wait_send()


def fused(grad_out, inputs, pre_first, pre_second, filter_first, filter_second):
    n = lax.axis_size("gx")
    xs, ys, zs, ch = grad_out.shape
    rows = filter_first.shape[0]
    if rows % sub or n % 4 or n < 8 or lax.axis_size("groups") != 2:
        return on_device(grad_out, inputs, pre_first, pre_second, filter_first, filter_second)
    units, hi, bf = rows // sub, n // 4, jnp.bfloat16
    dma = pltpu.SemaphoreType.DMA
    piece = (units, sub, ch)
    gin, own1, own2 = pl.pallas_call(
        functools.partial(kernel, n),
        out_shape=(
            jax.ShapeDtypeStruct(grad_out.shape, bf),
            jax.ShapeDtypeStruct(piece, jnp.float32),
            jax.ShapeDtypeStruct(piece, jnp.float32),
        ),
        in_specs=[pl.BlockSpec(memory_space=pltpu.VMEM)] * 6,
        out_specs=[pl.BlockSpec(memory_space=pltpu.VMEM)] * 3,
        scratch_shapes=[
            pltpu.VMEM((2, n * units, sub, ch), bf),
            pltpu.VMEM((2, 3 * ch, 9 * ch), bf),
            pltpu.VMEM((2, xs + 2, ys + 2, zs, ch), bf),
            pltpu.VMEM((xs, ys, zs, ch), bf),
            pltpu.VMEM((1, 2, ys, zs, ch), bf),
            pltpu.VMEM((2, xs + 2, ch, (ys + 2) * zs), bf),
            pltpu.VMEM((2, xs + 2, ys + 2, zs, 3 * ch), bf),
            pltpu.VMEM((xs, ys, zs, ch), jnp.float32),
            pltpu.VMEM((2, n * units, sub, ch), jnp.float32),
            pltpu.VMEM((2, 2, hi) + piece, bf),
            pltpu.VMEM((2, 2, hi) + piece, bf),
            pltpu.VMEM((2, hi) + piece, bf),
            pltpu.VMEM((2, hi) + piece, bf),
            pltpu.VMEM((2, hi) + piece, bf),
            pltpu.VMEM((2, hi) + piece, bf),
            dma((3, 2)), dma((3, 2)),
            dma((2, hi)), dma((2, hi)),
            dma((2, hi)), dma((2, hi)),
            dma((2, 2 * hi)), dma((2, 2 * hi)),
            dma((2, 2 * hi)), dma((2, 2 * hi)),
            dma((2, 2)), dma((2, 2)),
            dma((2, hi)), dma((2, hi)),
            dma((2, hi)), dma((2, hi)),
        ],
        compiler_params=pltpu.CompilerParams(collective_id=0, has_side_effects=True),
    )(
        grad_out, inputs, pre_first, pre_second,
        filter_first.reshape(piece), filter_second.reshape(piece),
    )
    return gin, own1.reshape(rows, ch), own2.reshape(rows, ch)


def solution(mesh):
    return jax.shard_map(
        fused,
        mesh=mesh,
        in_specs=(
            P(("groups", "gx"), None, None, None),
            P(("groups", "gx"), None, None, None),
            P(("groups", "gx"), None, None, None),
            P(("groups", "gx"), None, None, None),
            P("gx", None),
            P("gx", None),
        ),
        out_specs=(P(("groups", "gx"), None, None, None), P("gx", "groups"), P("gx", "groups")),
        check_vma=False,
    )
```

```python
import functools
import math

import jax
import jax.numpy as jnp
from jax import lax
from jax.experimental import pallas as pl
from jax.experimental.pallas import tpu as pltpu
from jax.sharding import PartitionSpec as P

inv_root_two = 0.7071067811865476
inv_root_twopi = 0.3989422804014327
tap_shifts = ((-1, -1), (-1, 0), (-1, 1), (0, -1), (0, 0), (0, 1), (1, -1), (1, 0), (1, 1))


def with_halo(block, sides, width):
    for axis, dim in sides:
        count = lax.axis_size(axis)
        forward = [(i, i + 1) for i in range(count - 1)]
        backward = [(target, source) for source, target in forward]
        low = lax.ppermute(
            lax.slice_in_dim(block, block.shape[dim] - width, None, axis=dim), axis, forward
        )
        high = lax.ppermute(lax.slice_in_dim(block, 0, width, axis=dim), axis, backward)
        block = jnp.concatenate([low, block, high], axis=dim)
    return block


def gelu_parts(value):
    normal_cdf = 0.5 * (1.0 + lax.erf(value * inv_root_two))
    return (value * normal_cdf, normal_cdf + value * jnp.exp(-0.5 * value * value) * inv_root_twopi)


def pad_sides(extended):
    return jnp.pad(extended, ((0, 0), (1, 1), (1, 1), (0, 0)))


def stack_taps(padded, direction, z_cells):
    return jnp.concatenate(
        [
            padded[:, :, 1 + direction * shift_z : 1 + direction * shift_z + z_cells]
            for shift_z in (-1, 0, 1)
        ],
        axis=3,
    )


def window(stacked, direction, shift_x, shift_y, x_cells, y_cells):
    start_x = 1 + direction * shift_x
    start_y = 1 + direction * shift_y
    return stacked[start_x : start_x + x_cells, start_y : start_y + y_cells]


def back_data(stacked, full_filter, shape):
    x_cells, y_cells, z_cells, channels = shape
    kernel = full_filter.reshape(3, 3, 3, channels, channels)
    running = jnp.zeros((x_cells * y_cells * z_cells, channels), jnp.float32)
    for shift_x, shift_y in tap_shifts:
        tap_matrix = jnp.transpose(kernel[shift_x + 1, shift_y + 1], (0, 2, 1)).reshape(
            3 * channels, channels
        )
        piece = window(stacked, -1, shift_x, shift_y, x_cells, y_cells).reshape(-1, 3 * channels)
        running = running + jnp.dot(piece, tap_matrix, preferred_element_type=jnp.float32)
    return running.reshape(shape)


def filter_from_inputs(stacked, grads, shape):
    x_cells, y_cells, z_cells, channels = shape
    flat_grads = grads.reshape(-1, channels)
    blocks = []
    for shift_x, shift_y in tap_shifts:
        piece = window(stacked, 1, shift_x, shift_y, x_cells, y_cells).reshape(-1, 3 * channels)
        product = lax.dot_general(
            piece, flat_grads, (((0,), (0,)), ((), ())), preferred_element_type=jnp.float32
        )
        blocks.append(product.reshape(3, channels, channels))
    return jnp.stack(blocks).reshape(27 * channels, channels)


def on_device(grad_out, inputs, pre_first, pre_second, filter_first, filter_second):
    shape = grad_out.shape
    x_cells, y_cells, z_cells, channels = shape
    full_first, full_second = (
        lax.all_gather(filter_first, "gx", axis=0, tiled=True),
        lax.all_gather(filter_second, "gx", axis=0, tiled=True),
    )
    grad_scale = 1.0 / math.sqrt(x_cells * lax.axis_size("gx") * y_cells * z_cells)
    unused_value, slope_two = gelu_parts(pre_second.astype(jnp.float32))
    grad_two = (grad_out.astype(jnp.float32) * slope_two).astype(jnp.bfloat16)
    act_one, slope_one = gelu_parts(pre_first.astype(jnp.float32))
    act_one = act_one.astype(jnp.bfloat16)
    extended_two = pad_sides(with_halo(grad_two, (("gx", 0),), 1))
    stacked_two = stack_taps(extended_two, -1, z_cells)
    grad_act = back_data(stacked_two, full_second, shape)
    extended_act = pad_sides(with_halo(act_one, (("gx", 0),), 1))
    filt_two = filter_from_inputs(stack_taps(extended_act, 1, z_cells), grad_two, shape)
    owned_two = lax.psum_scatter(filt_two * grad_scale, "gx", scatter_dimension=0, tiled=True)
    grad_one = (grad_act * slope_one).astype(jnp.bfloat16)
    extended_one = pad_sides(with_halo(grad_one, (("gx", 0),), 1))
    stacked_one = stack_taps(extended_one, -1, z_cells)
    grad_in = back_data(stacked_one, full_first, shape).astype(jnp.bfloat16)
    extended_in = pad_sides(with_halo(inputs, (("gx", 0),), 1))
    filt_one = filter_from_inputs(stack_taps(extended_in, 1, z_cells), grad_one, shape)
    owned_one = lax.psum_scatter(filt_one * grad_scale, "gx", scatter_dimension=0, tiled=True)
    return (grad_in, owned_one, owned_two)


MESH = pl.DeviceIdType.MESH
sub = 8


def shift_z(block, shift):
    if shift == 0:
        return block
    cells = block.shape[0]
    row = lax.broadcasted_iota(jnp.int32, block.shape, 0)
    edge = 0 if shift > 0 else cells - 1
    return jnp.where(row == edge, 0.0, pltpu.roll(block, shift % cells, 0))


def kernel(
    n, go, xin, p1, p2, f1, f2, gin, own1, own2,
    fbuf, wbuf, gext, abuf, ahalo, sat, gcat, slope, part, s1, r1, s2, r2, s3, r3,
    halo_s, halo_r, agz_s, agz_r, agx_s, agx_r, agy_s, agy_r, agc_s, agc_r,
    rs1_s, rs1_r, rs2_s, rs2_r, rs3_s, rs3_r,
):
    xs, ys, zs, ch = go.shape
    units = f1.shape[0]
    hi = n // 4
    group, me = lax.axis_index("groups"), lax.axis_index("gx")
    core = me % 2
    mid = (me // 2) % 2
    top = me // 4
    partner = me + 1 - 2 * core
    across = me + 2 - 4 * mid

    def owner(t, m, c):
        return (t * 2 + m) * 2 + c

    def chunk(t, m, c):
        return pl.ds(owner(t, m, c) * units, units)

    def ahead(d):
        return lax.rem(top + d, hi)

    def behind(d):
        return lax.rem(top + hi - d, hi)

    lead = core == group
    sent = []

    def push(src, dst, send, recv, target, plane=group, keep=True):
        copy = pltpu.make_async_remote_copy(
            src_ref=src, dst_ref=dst, send_sem=send, recv_sem=recv,
            device_id=(plane, target), device_id_type=MESH,
        )
        copy.start()
        if keep:
            sent.append(copy)

    def arrive(dst, send, recv):
        pltpu.make_async_remote_copy(
            src_ref=dst, dst_ref=dst, send_sem=send, recv_sem=recv,
            device_id=(group, partner), device_id_type=MESH,
        ).wait_recv()

    barrier = pltpu.get_barrier_semaphore()
    peers = [partner, across, lax.rem(me + 1, n), lax.rem(me + n - 1, n)]
    peers += [owner(ahead(d), mid, core) for d in range(1, hi)]
    for peer in peers:
        pl.semaphore_signal(barrier, inc=1, device_id=(group, peer), device_id_type=MESH)
    pl.semaphore_signal(barrier, inc=1, device_id=(1 - group, me), device_id_type=MESH)
    pl.semaphore_wait(barrier, len(peers) + 1)

    filters = (f2, f1)

    def when_relay(f):
        return pl.when(lead) if f else lambda run: run()

    def gather_own(f):
        mine = fbuf.at[f, chunk(top, mid, core)]
        src = filters[f]
        push(src, mine, agc_s.at[f, 0], agc_r.at[f, 0], partner)

        @when_relay(f)
        def _():
            for d in range(1, hi):
                push(
                    src, mine, agz_s.at[f, d], agz_r.at[f, d],
                    owner(ahead(d), mid, core), keep=False,
                )
            push(src, mine, agx_s.at[f, 0], agx_r.at[f, 0], across, keep=False)

        fbuf[f, chunk(top, mid, core)] = src[...]

    def hand_on(f, got, k):
        if f:
            push(got, got, agy_s.at[f, k], agy_r.at[f, k], me, 1 - group, False)
        push(got, got, agc_s.at[f, k], agc_r.at[f, k], partner, keep=False)

    def gather_top(f):
        @when_relay(f)
        def _():
            for d in range(1, hi):
                got = fbuf.at[f, chunk(behind(d), mid, core)]
                arrive(got, agz_s.at[f, d], agz_r.at[f, d])
                push(got, got, agx_s.at[f, d], agx_r.at[f, d], across, keep=False)
                hand_on(f, got, d)

    def gather_mid(f):
        @when_relay(f)
        def _():
            for d in range(hi):
                got = fbuf.at[f, chunk(behind(d), 1 - mid, core)]
                arrive(got, agx_s.at[f, d], agx_r.at[f, d])
                hand_on(f, got, hi + d)

    def gather_follow(f):
        @pl.when(jnp.logical_not(lead))
        def _():
            for k in range(1, 2 * hi):
                which = mid if k < hi else 1 - mid
                got = fbuf.at[f, chunk(behind(k % hi), which, core)]
                arrive(got, agy_s.at[f, k], agy_r.at[f, k])
                push(got, got, agc_s.at[f, k], agc_r.at[f, k], partner, keep=False)

    def gather_core(f):
        for m in range(2):
            for d in range(hi):
                which = mid if m == 0 else 1 - mid
                got = fbuf.at[f, chunk(behind(d), which, 1 - core)]
                arrive(got, agc_s.at[f, m * hi + d], agc_r.at[f, m * hi + d])
        taps = 3 * ch // sub
        for ab in range(9):
            rows = fbuf[f, ab * taps : (ab + 1) * taps].astype(jnp.float32)
            wbuf[f, :, ab * ch : (ab + 1) * ch] = rows.reshape(3 * ch, ch).astype(jnp.bfloat16)

    def halo_copy(h, first, last, low, high):
        to_left = pltpu.make_async_remote_copy(
            src_ref=first, dst_ref=high, send_sem=halo_s.at[h, 0], recv_sem=halo_r.at[h, 1],
            device_id=(group, lax.rem(me + n - 1, n)), device_id_type=MESH,
        )
        to_right = pltpu.make_async_remote_copy(
            src_ref=last, dst_ref=low, send_sem=halo_s.at[h, 1], recv_sem=halo_r.at[h, 0],
            device_id=(group, lax.rem(me + 1, n)), device_id_type=MESH,
        )

        @pl.when(me > 0)
        def _():
            to_left.start()

        @pl.when(me < n - 1)
        def _():
            to_right.start()

        return to_left, to_right, low, high, h

    def halo_wait(halo):
        _, _, low, high, h = halo

        @pl.when(me > 0)
        def _():
            arrive(low, halo_s.at[h, 0], halo_r.at[h, 0])

        @pl.when(me == 0)
        def _():
            low[...] = jnp.zeros(low.shape, low.dtype)

        @pl.when(me < n - 1)
        def _():
            arrive(high, halo_s.at[h, 1], halo_r.at[h, 1])

        @pl.when(me == n - 1)
        def _():
            high[...] = jnp.zeros(high.shape, high.dtype)

    def grad_halo(h, f):
        inner = pl.ds(1, ys)
        return halo_copy(
            h, gext.at[f, 1, inner], gext.at[f, xs, inner],
            gext.at[f, 0, inner], gext.at[f, xs + 1, inner],
        )

    def saved_halo(h, s, block):
        return halo_copy(h, block.at[0], block.at[xs - 1], ahalo.at[s, 0], ahalo.at[s, 1])

    def keep_shifts(f, x, y, value):
        for c in (-1, 0, 1):
            gcat[f, x + 1, y + 1, :, (c + 1) * ch : (c + 2) * ch] = shift_z(value, c).astype(
                jnp.bfloat16
            )

    def keep_grad(f, x, y, value):
        gext[f, x + 1, y + 1] = value.astype(jnp.bfloat16)
        keep_shifts(f, x, y, value)

    def halo_shifts(f):
        for x in (-1, xs):
            for y in range(ys):
                keep_shifts(f, x, y, gext[f, x + 1, y + 1].astype(jnp.float32))

    def turn(s, layer, block):
        for y in range(ys):
            sat[s, layer, :, (y + 1) * zs : (y + 2) * zs] = block[y].T

    def filter_terms(s):
        for a in range(3):
            lhs = jnp.concatenate(
                [
                    jnp.concatenate(
                        [sat[s, x + a, :, b * zs : (b + ys) * zs] for x in range(xs)], axis=1
                    )
                    for b in range(3)
                ],
                axis=0,
            )
            rhs = gcat[s, 1 : xs + 1, 1 : ys + 1].reshape(xs * ys * zs, 3 * ch)
            out = jnp.dot(lhs, rhs, preferred_element_type=jnp.float32)
            per = ch // sub
            for b in range(3):
                for c in range(3):
                    at = (9 * a + 3 * b + c) * per
                    part[s, at : at + per] = out[
                        b * ch : (b + 1) * ch, c * ch : (c + 1) * ch
                    ].reshape(per, sub, ch)

    def filter_terms_halo(s):
        lhs = jnp.concatenate([sat[s, x + 1, :, zs : (ys + 1) * zs] for x in range(xs)], axis=1)
        per = ch // sub
        for a in (0, -1, 1):
            for b in (-1, 0, 1):
                rhs = gcat[s, 1 - a : 1 - a + xs, 1 - b : 1 - b + ys].reshape(
                    xs * ys * zs, 3 * ch
                )
                out = jnp.dot(lhs, rhs, preferred_element_type=jnp.float32)
                for c in range(3):
                    at = (9 * (a + 1) + 3 * (b + 1) + c) * per
                    part[s, at : at + per] = out[:, c * ch : (c + 1) * ch].reshape(per, sub, ch)

    def scatter_core(s):
        for m in range(2):
            which = 1 - mid if m == 0 else mid
            for t in range(hi):
                s1[s, m, t] = part[s, chunk(t, which, 1 - core)].astype(jnp.bfloat16)
            push(s1.at[s, m], r1.at[s, m], rs1_s.at[s, m], rs1_r.at[s, m], partner)

    def scatter_mid(s):
        arrive(r1.at[s, 0], rs1_s.at[s, 0], rs1_r.at[s, 0])
        for d in [*range(1, hi), 0]:
            t = ahead(d)
            s2[s, t] = (
                part[s, chunk(t, 1 - mid, core)] + r1[s, 0, t].astype(jnp.float32)
            ).astype(jnp.bfloat16)
            push(s2.at[s, t], r2.at[s, t], rs2_s.at[s, d], rs2_r.at[s, d], across)

    def total(s, t):
        return (
            part[s, chunk(t, mid, core)]
            + r1[s, 1, t].astype(jnp.float32)
            + r2[s, t].astype(jnp.float32)
        )

    def scatter_top(s):
        arrive(r1.at[s, 1], rs1_s.at[s, 1], rs1_r.at[s, 1])
        for d in range(1, hi):
            arrive(r2.at[s, ahead(d)], rs2_s.at[s, d], rs2_r.at[s, d])
            s3[s, d] = total(s, ahead(d)).astype(jnp.bfloat16)
            push(
                s3.at[s, d], r3.at[s, d], rs3_s.at[s, d], rs3_r.at[s, d],
                owner(ahead(d), mid, core),
            )

    def scatter_end(s, out):
        arrive(r2.at[s, top], rs2_s.at[s, 0], rs2_r.at[s, 0])
        value = total(s, top)
        for d in range(1, hi):
            arrive(r3.at[s, d], rs3_s.at[s, d], rs3_r.at[s, d])
            value = value + r3[s, d].astype(jnp.float32)
        out[...] = value

    def layer_back(f, x):
        lhs = jnp.concatenate(
            [
                gext[f, x + 1 - a, 1 - b : 1 - b + ys].reshape(ys * zs, ch)
                for a in (-1, 0, 1)
                for b in (-1, 0, 1)
            ],
            axis=1,
        )
        wide = lax.dot_general(
            lhs, wbuf[f], (((1,), (1,)), ((), ())), preferred_element_type=jnp.float32
        )
        rows = []
        for y in range(ys):
            block = wide[y * zs : (y + 1) * zs]
            rows.append(
                shift_z(block[:, :ch], -1) + block[:, ch : 2 * ch] + shift_z(block[:, 2 * ch :], 1)
            )
        return rows

    gather_own(0)
    halo_in = saved_halo(0, 0, xin)
    gather_own(1)

    for f in range(2):
        for x in range(xs + 2):
            for y in (0, ys + 1):
                gext[f, x, y] = jnp.zeros((zs, ch), jnp.bfloat16)
                gcat[f, x, y] = jnp.zeros((zs, 3 * ch), jnp.bfloat16)
                sat[f, x, :, y * zs : (y + 1) * zs] = jnp.zeros((ch, zs), jnp.bfloat16)

    @pl.loop(0, xs * ys)
    def _(i):
        x, y = i // ys, i % ys
        _, slope_two = gelu_parts(p2[x, y].astype(jnp.float32))
        keep_grad(0, x, y, go[x, y].astype(jnp.float32) * slope_two)
        act, slope_one = gelu_parts(p1[x, y].astype(jnp.float32))
        abuf[x, y] = act.astype(jnp.bfloat16)
        slope[x, y] = slope_one

    halo_two = grad_halo(1, 0)
    gather_top(0)
    for x in range(xs):
        turn(0, x + 1, abuf[x])
        turn(1, x + 1, xin[x])
    gather_mid(0)
    halo_wait(halo_two)
    halo_shifts(0)
    filter_terms_halo(0)
    scatter_core(0)
    gather_core(0)
    gather_top(1)
    scatter_mid(0)
    for x in range(xs):
        for y, value in enumerate(layer_back(0, x)):
            keep_grad(1, x, y, value * slope[x, y])
    halo_wait(halo_in)
    turn(1, 0, ahalo[0, 0])
    turn(1, xs + 1, ahalo[0, 1])
    filter_terms(1)
    scatter_core(1)
    scatter_mid(1)
    halo_one = grad_halo(2, 1)
    gather_mid(1)
    scatter_top(0)
    gather_follow(1)
    scatter_top(1)
    gather_core(1)
    halo_wait(halo_one)
    for x in range(xs):
        for y, value in enumerate(layer_back(1, x)):
            gin[x, y] = value
    scatter_end(0, own2)
    scatter_end(1, own1)
    for copy in sent:
        copy.wait_send()

    def left(f, send):
        pltpu.make_async_remote_copy(
            src_ref=filters[f], dst_ref=filters[f], send_sem=send, recv_sem=agc_r.at[f, 0],
            device_id=(group, partner), device_id_type=MESH,
        ).wait_send()

    for f in range(2):
        for k in range(1, 2 * hi):
            left(f, agc_s.at[f, k])

    for f in range(2):

        @when_relay(f)
        def _():
            for d in range(1, hi):
                left(f, agz_s.at[f, d])
            for d in range(hi):
                left(f, agx_s.at[f, d])
            if f:
                for k in range(1, 2 * hi):
                    left(f, agy_s.at[f, k])

    for halo in (halo_two, halo_in, halo_one):

        @pl.when(me > 0)
        def _():
            halo[0].wait_send()

        @pl.when(me < n - 1)
        def _():
            halo[1].wait_send()


def fused(grad_out, inputs, pre_first, pre_second, filter_first, filter_second):
    n = lax.axis_size("gx")
    xs, ys, zs, ch = grad_out.shape
    rows = filter_first.shape[0]
    if rows % sub or n % 4 or n < 8 or lax.axis_size("groups") != 2:
        return on_device(grad_out, inputs, pre_first, pre_second, filter_first, filter_second)
    units, hi, bf = rows // sub, n // 4, jnp.bfloat16
    dma = pltpu.SemaphoreType.DMA
    piece = (units, sub, ch)
    gin, own1, own2 = pl.pallas_call(
        functools.partial(kernel, n),
        out_shape=(
            jax.ShapeDtypeStruct(grad_out.shape, jnp.float32),
            jax.ShapeDtypeStruct(piece, jnp.float32),
            jax.ShapeDtypeStruct(piece, jnp.float32),
        ),
        in_specs=[pl.BlockSpec(memory_space=pltpu.VMEM)] * 6,
        out_specs=[pl.BlockSpec(memory_space=pltpu.VMEM)] * 3,
        scratch_shapes=[
            pltpu.VMEM((2, n * units, sub, ch), bf),
            pltpu.VMEM((2, 3 * ch, 9 * ch), bf),
            pltpu.VMEM((2, xs + 2, ys + 2, zs, ch), bf),
            pltpu.VMEM((xs, ys, zs, ch), bf),
            pltpu.VMEM((1, 2, ys, zs, ch), bf),
            pltpu.VMEM((2, xs + 2, ch, (ys + 2) * zs), bf),
            pltpu.VMEM((2, xs + 2, ys + 2, zs, 3 * ch), bf),
            pltpu.VMEM((xs, ys, zs, ch), jnp.float32),
            pltpu.VMEM((2, n * units, sub, ch), jnp.float32),
            pltpu.VMEM((2, 2, hi) + piece, bf),
            pltpu.VMEM((2, 2, hi) + piece, bf),
            pltpu.VMEM((2, hi) + piece, bf),
            pltpu.VMEM((2, hi) + piece, bf),
            pltpu.VMEM((2, hi) + piece, bf),
            pltpu.VMEM((2, hi) + piece, bf),
            dma((3, 2)), dma((3, 2)),
            dma((2, hi)), dma((2, hi)),
            dma((2, hi)), dma((2, hi)),
            dma((2, 2 * hi)), dma((2, 2 * hi)),
            dma((2, 2 * hi)), dma((2, 2 * hi)),
            dma((2, 2)), dma((2, 2)),
            dma((2, hi)), dma((2, hi)),
            dma((2, hi)), dma((2, hi)),
        ],
        compiler_params=pltpu.CompilerParams(collective_id=0, has_side_effects=True),
    )(
        grad_out, inputs, pre_first, pre_second,
        filter_first.reshape(piece), filter_second.reshape(piece),
    )
    scale = 1.0 / math.sqrt(xs * n * ys * zs)
    return gin.astype(bf), own1.reshape(rows, ch) * scale, own2.reshape(rows, ch) * scale


def solution(mesh):
    return jax.shard_map(
        fused,
        mesh=mesh,
        in_specs=(
            P(("groups", "gx"), None, None, None),
            P(("groups", "gx"), None, None, None),
            P(("groups", "gx"), None, None, None),
            P(("groups", "gx"), None, None, None),
            P("gx", None),
            P("gx", None),
        ),
        out_specs=(P(("groups", "gx"), None, None, None), P("gx", "groups"), P("gx", "groups")),
        check_vma=False,
    )
```
